256 devices in a mesh: dp: 32 (over y, z), vocab: 8 (over x, core).
Axes of the slice: x: 4, y: 4, z: 8, core: 2. Of those that a mesh axis runs over, the one named last changes fastest.
Arguments:
- draft_logits: bfloat16 [4096, 128000], P('dp', 'vocab'), may hold values from -15 to 250
- hidden: bfloat16 [4096, 2304], P('dp'), may hold values from -40 to 40
- embed_cot: bfloat16 [4096, 2304], P('dp'), may hold values from -0.59765625 to 0.59765625
- draft_ids: int32 [4096], P('dp'), may hold values from 0 to 127999, as said below
- target_ids: int32 [4096, 32], P('dp'), may hold values from 0 to 128255
- target_logits: float32 [4096, 32], P('dp'), may hold values from -8 to 240
- vocab_map: int32 [128256], replicated, may hold values from 0 to 127999
- master: float32 [128000, 2304], P(('vocab', 'dp')), may hold values from -6 to 6
- row_moment: float32 [128000], P(('vocab', 'dp')), may hold values from 0.0001 to 0.5
- col_moment: float32 [2304], replicated, may hold values from 0.003 to 0.03
Outputs:
- direction: bfloat16 [128000, 2304], P(('vocab', 'dp'))
- row_new: float32 [128000], P(('vocab', 'dp'))
- col_new: float32 [2304], replicated
- next_rows: bfloat16 [4096, 2304], P('dp')
The draws below stay inside these ranges and needn't reach their ends.
Inputs may be any that keep to these rules, and one draw needn't show every extreme that they name: `draft_ids`: among the 128 tokens of one index of dp, at most 20 have draft ids in any one block of 16000 consecutive ids, and some block holds exactly 20 of them.
All inputs are finite; a program needn't handle non-finite values.
Results may differ from the reference program's by a relative error of at most 0.0073.
Values may be sent and summed in bfloat16 or wider, within the bound.
No kernel may reach another device: no remote copies, remote signals or barrier semaphores. Data moves between devices by JAX's collectives and lax.ppermute only.
A program may use at most 128 MiB of HBM per device.

```python
import math
import jax
import jax.numpy as jnp
from jax import lax

D = 2304
TARGET_VOCAB = 128256
TOPK = 32
TOK_DEV = 128
SHARD_ROWS = 16000
VOCAB = 128000
TOKENS = 4096
SLOTS = 20
N_VOCAB = 8


def draw_draft_ids(key, part):
    vocab_count = VOCAB // SHARD_ROWS
    dp_count = TOKENS // TOK_DEV
    slot_total = vocab_count * SLOTS

    def one_block(block_key):
        first_key, second_key, third_key, fourth_key = jax.random.split(block_key, 4)
        chosen = jax.random.randint(first_key, (), 0, vocab_count)
        ranking = jax.random.permutation(second_key, slot_total)
        shard_of = jnp.arange(slot_total, dtype=jnp.int32) // SLOTS
        scores = ranking + jnp.where(shard_of == chosen, 0, slot_total)
        picked = jnp.argsort(scores, stable=True)[:TOK_DEV]
        shards = jax.random.permutation(third_key, shard_of[picked])
        offsets = jax.random.randint(fourth_key, (TOK_DEV,), 0, SHARD_ROWS)
        return (shards * SHARD_ROWS + offsets).astype(jnp.int32)
    block_keys = jax.random.split(jax.random.fold_in(key, 11), dp_count)
    return jax.vmap(one_block)(block_keys).reshape(TOKENS)


def draw_vocab_map(key, part):
    first_key, second_key = jax.random.split(jax.random.fold_in(key, 23))
    first = jax.random.randint(first_key, (TARGET_VOCAB,), 0, VOCAB)
    second = jax.random.randint(second_key, (TARGET_VOCAB,), 0, VOCAB)
    return jnp.maximum(first, second).astype(jnp.int32)


def draw_draft_logits(key, part):
    base_key = jax.random.fold_in(key, 37)
    return jnp.clip(2.5 * jax.random.normal(base_key, (TOKENS, VOCAB), jnp.float32), -15.0, 15.0).astype(jnp.bfloat16)


def draw_target_logits(key, part):
    base_key = jax.random.fold_in(key, 41)
    return jnp.clip(2.0 * jax.random.normal(base_key, (TOKENS, TOPK), jnp.float32), -8.0, 8.0)


def draw_hidden(key, part):
    first_key, second_key, third_key = jax.random.split(jax.random.fold_in(key, 53), 3)
    row_scale = jnp.exp(jax.random.uniform(second_key, (TOKENS, 1), jnp.float32, -1.15, 1.15))
    col_scale = jnp.exp(jax.random.uniform(third_key, (1, D), jnp.float32, -1.15, 1.15))
    values = jax.random.normal(first_key, (TOKENS, D), jnp.float32) * row_scale * col_scale
    return jnp.clip(values, -40.0, 40.0).astype(jnp.bfloat16)


def draw_row_moment(key, part):
    level = jax.random.uniform(jax.random.fold_in(key, 67), (VOCAB,), jnp.float32, math.log(0.0001), math.log(0.1))
    rising = 1.0 + 2.0 * jnp.arange(VOCAB, dtype=jnp.float32) / VOCAB
    return jnp.clip(jnp.exp(level) * rising, 0.0001, 0.5)


def place_ends(values, key, smallest, largest):
    extent = values.shape
    spot = [jax.random.randint(jax.random.fold_in(key, axis), (), 0, extent[axis]) for axis in range(len(extent))]
    values = values.at[tuple(spot)].set(smallest)
    longest = extent.index(max(extent))
    spot[longest] = (spot[longest] + 1) % extent[longest]
    return values.at[tuple(spot)].set(largest)


def block_levels(key, shape, pieces, low, top_value):
    loudness = 1.0
    for position, shards_of in pieces:
        heights = jax.random.uniform(jax.random.fold_in(jax.random.fold_in(key, 6), position), (shards_of,), jnp.float32, low / len(pieces), top_value / len(pieces))
        loudness = loudness * jnp.repeat(jnp.exp(heights), shape[position] // shards_of).reshape((-1,) + (1,) * (len(shape) - 1 - position))
    return loudness


def bell_draw(key, shape, scale, limit, cuts=(), held_as=jnp.bfloat16):
    level = block_levels(key, shape, cuts, -0.22, 0.18) if cuts else 1.0
    values = jax.random.normal(key, shape, jnp.float32) * scale * level
    return jnp.minimum(jnp.maximum(values, -limit), limit).astype(held_as)


def setup_inputs(seed: int = 0) -> dict:
    arg_keys = jax.random.split(jax.random.key(seed), 11)
    return {
        "draft_logits": draw_draft_logits(jax.random.fold_in(arg_keys[10], 71), 0),
        "hidden": draw_hidden(jax.random.fold_in(arg_keys[10], 71), 0),
        "embed_cot": bell_draw(arg_keys[2], (TOKENS, D), 0.1, 0.59765625, ((0, 32),)),
        "draft_ids": draw_draft_ids(jax.random.fold_in(arg_keys[10], 71), 0),
        "target_ids": place_ends(jax.random.randint(arg_keys[4], (TOKENS, TOPK), 0, TARGET_VOCAB), jax.random.fold_in(arg_keys[4], 1), 0, TARGET_VOCAB - 1).astype(jnp.int32),
        "target_logits": draw_target_logits(jax.random.fold_in(arg_keys[10], 71), 0),
        "vocab_map": draw_vocab_map(jax.random.fold_in(arg_keys[10], 71), 0),
        "master": bell_draw(arg_keys[7], (VOCAB, D), 1.0, 6.0, ((0, 256),), jnp.float32),
        "row_moment": draw_row_moment(jax.random.fold_in(arg_keys[10], 71), 0),
        "col_moment": jnp.clip(jnp.exp(jax.random.uniform(arg_keys[9], (D,), jnp.float32, math.log(0.003), math.log(0.03))), 0.003, 0.03),
    }


DECAY_RATE = 0.9
STEP_SCALE = 0.01
SQUARE_EPS = 1e-30

def block_columns(values, block_index, breadth):
    return lax.dynamic_slice_in_dim(values, block_index * breadth, breadth, 1)

def reference(draft_logits, hidden, embed_cot, draft_ids, target_ids, target_logits, vocab_map, master, row_moment, col_moment):
    breadth = SHARD_ROWS
    block_list = jnp.arange(N_VOCAB, dtype=jnp.int32)

    def block_max(block_index):
        return lax.optimization_barrier(jnp.max(block_columns(draft_logits, block_index, breadth).astype(jnp.float32), axis=1))
    highest = lax.optimization_barrier(jnp.max(lax.map(block_max, block_list), axis=0))

    def block_total(block_index):
        segment = block_columns(draft_logits, block_index, breadth).astype(jnp.float32)
        return lax.optimization_barrier(jnp.sum(jnp.exp(segment - highest[:, None]), axis=1))
    totals = lax.optimization_barrier(jnp.sum(lax.map(block_total, block_list), axis=0))
    shifted = target_logits - lax.optimization_barrier(jnp.max(target_logits, axis=1, keepdims=True))
    target_exp = jnp.exp(shifted)
    weights = target_exp / lax.optimization_barrier(jnp.sum(target_exp, axis=1, keepdims=True))
    mapped = vocab_map[target_ids]
    token_index = jnp.broadcast_to(jnp.arange(TOKENS, dtype=jnp.int32)[:, None], target_ids.shape)
    hidden_wide = hidden.astype(jnp.float32)
    cot_wide = embed_cot.astype(jnp.float32)

    def block_grad(block_index):
        begin_col = (block_index * breadth).astype(jnp.int32)
        segment = block_columns(draft_logits, block_index, breadth).astype(jnp.float32)
        probs = jnp.exp(segment - highest[:, None]) / totals[:, None]
        local = mapped - begin_col
        inside = (local >= 0) & (local < breadth)
        target = jnp.zeros((TOKENS, breadth), jnp.float32).at[token_index, jnp.clip(local, 0, breadth - 1)].add(jnp.where(inside, weights, jnp.zeros_like(weights)))
        slopes = lax.optimization_barrier((probs - target).astype(jnp.bfloat16)).astype(jnp.float32)
        head_part = jnp.einsum('tv,td->vd', slopes, hidden_wide, precision=lax.Precision.HIGHEST)
        embed_local = draft_ids - begin_col
        embed_inside = (embed_local >= 0) & (embed_local < breadth)
        segments = jnp.where(embed_inside, embed_local, breadth).astype(jnp.int32)
        embed_part = jax.ops.segment_sum(cot_wide, segments, num_segments=breadth + 1)[:breadth]
        return head_part + embed_part
    grad = lax.map(block_grad, block_list).reshape(VOCAB, D)
    squares = grad * grad + SQUARE_EPS
    row_new = DECAY_RATE * row_moment + (1.0 - DECAY_RATE) * lax.optimization_barrier(jnp.mean(squares, axis=1))
    col_new = DECAY_RATE * col_moment + (1.0 - DECAY_RATE) * lax.optimization_barrier(jnp.mean(squares, axis=0))
    scale = row_new[:, None] * col_new[None, :] / jnp.mean(row_new)
    direction = grad / jnp.sqrt(scale)
    fresh = (master - STEP_SCALE * direction).astype(jnp.bfloat16)
    return (direction.astype(jnp.bfloat16), row_new, col_new, fresh[draft_ids])
```

```python
import functools

import jax
import jax.numpy as jnp
from jax import lax
from jax.experimental import pallas as pl
from jax.experimental.pallas import tpu as pltpu
from jax.sharding import Mesh
from jax.sharding import PartitionSpec as P

DECAY_RATE = 0.9
STEP_SCALE = 0.01
SQUARE_EPS = 1e-30
LANES = 128
DP = ("y", "z")
VOCAB = ("x", "c")
BF16 = jnp.bfloat16
F32 = jnp.float32
VMEM_BYTES = 56 * 1024 * 1024


def stats_kernel(logits_ref, out_ref):
    tokens, cols = logits_ref.shape
    chunks = cols // LANES

    def chunk(i):
        return logits_ref[:, pl.ds(pl.multiple_of(i * LANES, LANES), LANES)].astype(F32)

    running = lax.fori_loop(
        1, chunks, lambda i, m: jnp.maximum(m, chunk(i)), chunk(0), unroll=4
    )
    top = jnp.max(running, axis=1, keepdims=True)
    total = lax.fori_loop(
        0,
        chunks,
        lambda i, s: s + jnp.exp(chunk(i) - top),
        jnp.zeros((tokens, LANES), F32),
        unroll=5,
    )
    total = jnp.sum(total, axis=1, keepdims=True)
    lane = lax.broadcasted_iota(jnp.int32, (tokens, LANES), 1)
    out_ref[...] = jnp.where(lane == 0, top, total).T[0:8, :]


def slopes_kernel(
    wanted_ref, logits_ref, stats_ref, high_ref, low_ref, weight_ref, out_ref, target, flipped, stage
):
    tokens, cols = logits_ref.shape
    dests, sent_rows, _ = out_ref.shape
    slots = wanted_ref.shape[0] // dests
    owned = cols // dests
    used = sent_rows - owned
    chunks = cols // LANES
    row = lax.broadcasted_iota(jnp.int32, (LANES, LANES), 0)

    def build(t, carry):
        high = high_ref[pl.ds(t, 1), :]
        low = low_ref[pl.ds(t, 1), :]
        weight = weight_ref[pl.ds(t, 1), :]
        left = jnp.where(high == row, weight, 0.0).astype(BF16)
        right = jnp.where(low == row, 1.0, 0.0).astype(BF16)
        target[pl.ds(pl.multiple_of(t * LANES, LANES), LANES), :] = lax.dot_general(
            left, right, (((1,), (1,)), ((), ())), preferred_element_type=F32
        )
        return carry

    lax.fori_loop(0, tokens, build, 0, unroll=4)

    stats = stats_ref[...]
    tops = stats[:, 0, :]
    sums = stats[:, 1, :]
    highest = jnp.max(tops, axis=0, keepdims=True)
    totals = jnp.sum(sums * jnp.exp(tops - highest), axis=0, keepdims=True)
    columns = jnp.where(row == 0, highest, 1.0 / totals).T
    highest_col = jnp.broadcast_to(columns[:, 0:1], (tokens, LANES))
    inverse_col = jnp.broadcast_to(columns[:, 1:2], (tokens, LANES))

    def slope(i, carry):
        start = pl.multiple_of(i * LANES, LANES)
        values = logits_ref[:, pl.ds(start, LANES)].astype(F32)
        goal = target[pl.ds(i, tokens, stride=LANES), :]
        flipped[pl.ds(start, LANES), :] = (jnp.exp(values - highest_col) * inverse_col - goal).T
        return carry

    lax.fori_loop(0, chunks, slope, 0)

    def arrange(d, carry):
        stage[0 : owned + 4, :] = flipped[pl.ds(d * owned, owned + 4), :]
        for j in range(used):
            stage[owned + j : owned + j + 1, :] = flipped[pl.ds(wanted_ref[d * slots + j], 1), :]
        out_ref[d] = stage[...].astype(BF16)
        return carry

    lax.fori_loop(0, dests, arrange, 0)


def grad_kernel(
    parity_ref,
    slopes_ref,
    own_ref,
    other_ref,
    cot_ref,
    ids_ref,
    row_ids_ref,
    moment_ref,
    grad_ref,
    row_new_ref,
    sums_ref,
):
    step = pl.program_id(0)
    per_step, rows, tokens = slopes_ref.shape
    half = own_ref.shape[2]
    features = 2 * half
    owned = rows - 20
    own_at = pl.multiple_of(parity_ref[0] * half, LANES)
    other_at = pl.multiple_of((1 - parity_ref[0]) * half, LANES)

    @pl.when(step == 0)
    def _():
        match = jnp.where(ids_ref[0:1, :] == row_ids_ref[:, 0:1], 1.0, 0.0).astype(BF16)
        slots = cot_ref.shape[1] // 2
        wide = cot_ref.shape[0] * slots
        for side in range(2):
            cot = cot_ref[:, side * slots : (side + 1) * slots, :].reshape(wide, half)
            grad_ref[:, side * half : (side + 1) * half] = jnp.dot(
                match, cot, preferred_element_type=F32
            )

    left = jnp.concatenate([slopes_ref[j] for j in range(per_step)], axis=1)
    for ref, at in ((own_ref, own_at), (other_ref, other_at)):
        right = jnp.concatenate([ref[j] for j in range(per_step)], axis=0)
        grad_ref[:, pl.ds(at, half)] += jnp.dot(left, right, preferred_element_type=F32)

    @pl.when(step == pl.num_programs(0) - 1)
    def _():
        grad = grad_ref[...]
        squares = grad * grad + SQUARE_EPS
        mean = jnp.sum(squares, axis=1, keepdims=True) * (1.0 / features)
        row_new = DECAY_RATE * moment_ref[:, 0:1] + (1.0 - DECAY_RATE) * mean
        row_new_ref[...] = jnp.broadcast_to(row_new, row_new_ref.shape)
        is_owned = lax.broadcasted_iota(jnp.int32, (rows, 1), 0) < owned
        sums_ref[:, 0:features] = jnp.sum(
            jnp.where(is_owned, squares, 0.0), axis=0, keepdims=True
        )
        row_total = jnp.sum(jnp.where(is_owned, row_new, 0.0), axis=0, keepdims=True)
        sums_ref[:, features:] = jnp.broadcast_to(row_total, (1, LANES))


def total_over_all(value, sizes):
    for axis, size in sizes:
        step = 1
        while step < size:
            value = value + lax.ppermute(value, axis, [(i, i ^ step) for i in range(size)])
            step *= 2
    return value


def body(
    sizes,
    draft_logits,
    hidden,
    embed_cot,
    draft_ids,
    target_ids,
    target_logits,
    vocab_map,
    master,
    row_moment,
    col_moment,
):
    tokens, shard_cols = draft_logits.shape
    owned, features = master.shape
    topk = target_ids.shape[1]
    dp_y, dp_z = sizes["y"], sizes["z"]
    dp_count = dp_y * dp_z
    vocab_count = sizes["x"] * sizes["c"]
    parity = lax.axis_index("c")
    vocab_index = lax.axis_index("x") * sizes["c"] + parity
    dp_index = lax.axis_index("y") * dp_z + lax.axis_index("z")
    block_base = vocab_index * shard_cols
    row_base = (vocab_index * dp_count + dp_index) * owned
    half = features // 2
    used = tokens // vocab_count + tokens // (4 * vocab_count)
    slots = 32

    block_of = jnp.sum(
        (draft_ids[:, None] >= shard_cols * jnp.arange(1, vocab_count, dtype=jnp.int32)[None, :]),
        axis=1,
        dtype=jnp.int32,
    )
    place = jnp.arange(tokens, dtype=jnp.int32)
    slot_of = jnp.sum(
        (block_of[:, None] == block_of[None, :]) & (place[None, :] < place[:, None]),
        axis=1,
        dtype=jnp.int32,
    )
    placing = (slot_of[None, :] == jnp.arange(slots, dtype=jnp.int32)[:, None]) & (
        block_of == vocab_index
    )[None, :]
    filled = jnp.any(placing, axis=1)
    packed_ids = jnp.where(filled, jnp.sum(jnp.where(placing, draft_ids[None, :], 0), axis=1), -1)
    packed_cot = jnp.dot(placing.astype(BF16), embed_cot, preferred_element_type=F32).astype(BF16)

    hidden_half = lax.dynamic_slice_in_dim(hidden, parity * half, half, 1)
    to_gather = jnp.concatenate([hidden_half, packed_cot[:, :half], packed_cot[:, half:]], axis=0)
    own = lax.all_gather(to_gather, DP, axis=0)
    other = lax.ppermute(own, "c", [(0, 1), (1, 0)])

    all_ids = lax.all_to_all(
        jnp.broadcast_to(jnp.pad(packed_ids, (0, LANES - slots))[None, None, :], (dp_count, 8, LANES)),
        DP,
        0,
        0,
        tiled=True,
    )[:, 0, :slots]

    stats = pl.pallas_call(
        stats_kernel,
        out_shape=jax.ShapeDtypeStruct((8, LANES), F32),
        compiler_params=pltpu.CompilerParams(vmem_limit_bytes=VMEM_BYTES),
    )(draft_logits)
    all_stats = lax.all_to_all(
        jnp.broadcast_to(stats[None], (vocab_count, 8, LANES)), VOCAB, 0, 0, tiled=True
    )

    target_t = target_logits.T
    target_exp = jnp.exp(target_t - jnp.max(target_t, axis=0, keepdims=True))
    weights = target_exp / jnp.sum(target_exp, axis=0, keepdims=True)
    first = lax.reduce_precision(weights, 8, 7)
    second = lax.reduce_precision(weights - first, 8, 7)
    third = lax.reduce_precision(weights - first - second, 8, 7)
    mapped = vocab_map[target_ids.T] - block_base
    spare = jnp.zeros((LANES - 3 * topk, tokens), F32)
    weight_rows = jnp.concatenate([first, second, third, spare], axis=0).T
    mapped_rows = jnp.concatenate([mapped] * 3 + [jnp.full(spare.shape, -1, jnp.int32)], axis=0).T
    high_rows = mapped_rows >> 7
    low_rows = mapped_rows & (LANES - 1)

    wanted = jnp.where(all_ids >= 0, all_ids - block_base, 0)
    sent_rows = owned + used
    vmem = pl.BlockSpec(memory_space=pltpu.VMEM)
    slopes = pl.pallas_call(
        slopes_kernel,
        in_specs=[pl.BlockSpec(memory_space=pltpu.SMEM)] + [vmem] * 5,
        out_specs=vmem,
        out_shape=jax.ShapeDtypeStruct((dp_count, sent_rows, LANES), BF16),
        scratch_shapes=[
            pltpu.VMEM((tokens * LANES, LANES), F32),
            pltpu.VMEM((shard_cols + 8, LANES), F32),
            pltpu.VMEM((sent_rows, LANES), F32),
        ],
        compiler_params=pltpu.CompilerParams(vmem_limit_bytes=VMEM_BYTES),
    )(wanted.reshape(dp_count * slots), draft_logits, all_stats, high_rows, low_rows, weight_rows)
    owned_slopes = lax.all_to_all(slopes, DP, 0, 0, tiled=True)

    moment_1 = lax.reduce_precision(row_moment, 8, 7)
    moment_2 = lax.reduce_precision(row_moment - moment_1, 8, 7)
    moment_3 = lax.reduce_precision(row_moment - moment_1 - moment_2, 8, 7)
    moments = jnp.stack([moment_1, moment_2, moment_3], axis=1)
    master_wide = jnp.concatenate(
        [master.astype(BF16), jnp.pad(moments, ((0, 0), (0, LANES - 3))).astype(BF16)], axis=1
    )
    select = (
        all_ids[:, :used].reshape(-1)[:, None] - row_base
        == jnp.arange(owned, dtype=jnp.int32)[None, :]
    ).astype(BF16)
    picked = jnp.dot(select, master_wide, preferred_element_type=F32).astype(BF16)
    wide = features + LANES
    over_y = lax.all_to_all(picked.reshape(dp_y, dp_z * used, wide), "y", 0, 0, tiled=True)
    over_y = jnp.sum(over_y.astype(F32), axis=0).astype(BF16)
    over_z = lax.all_to_all(over_y.reshape(dp_z, used, wide), "z", 0, 0, tiled=True)
    mine = jnp.sum(over_z.astype(F32), axis=0)
    wanted_master = mine[:, :features]
    wanted_moment = mine[:, features] + mine[:, features + 1] + mine[:, features + 2]

    ids_lanes = jnp.where(
        jnp.arange(slots, dtype=jnp.int32)[None, :] < used, all_ids, -2
    ).reshape(1, dp_count * slots)
    row_ids = jnp.concatenate(
        [row_base + jnp.arange(owned, dtype=jnp.int32), packed_ids[:used]]
    )[:, None]
    moment_col = jnp.concatenate([row_moment, wanted_moment])[:, None]
    per_step = 4
    steps = dp_count // per_step
    resident = lambda shape: pl.BlockSpec(shape, lambda i: (0,) * len(shape))
    grad, row_new_all, sums = pl.pallas_call(
        grad_kernel,
        grid=(steps,),
        in_specs=[
            pl.BlockSpec(memory_space=pltpu.SMEM),
            pl.BlockSpec((per_step, sent_rows, LANES), lambda i: (i, 0, 0)),
            pl.BlockSpec((per_step, tokens, half), lambda i: (i, 0, 0)),
            pl.BlockSpec((per_step, tokens, half), lambda i: (i, 0, 0)),
            pl.BlockSpec((dp_count, 2 * slots, half), lambda i: (0, tokens // (2 * slots), 0)),
            resident((1, dp_count * slots)),
            resident((sent_rows, 1)),
            resident((sent_rows, 1)),
        ],
        out_specs=[
            resident((sent_rows, features)),
            resident((sent_rows, LANES)),
            resident((1, wide)),
        ],
        out_shape=[
            jax.ShapeDtypeStruct((sent_rows, features), F32),
            jax.ShapeDtypeStruct((sent_rows, LANES), F32),
            jax.ShapeDtypeStruct((1, wide), F32),
        ],
        compiler_params=pltpu.CompilerParams(
            dimension_semantics=("arbitrary",), vmem_limit_bytes=VMEM_BYTES
        ),
    )(parity.astype(jnp.int32).reshape(1), owned_slopes, own, other, own, ids_lanes, row_ids, moment_col)

    totals = total_over_all(
        sums, (("c", sizes["c"]), ("x", sizes["x"]), ("y", dp_y), ("z", dp_z))
    )
    vocab_rows = owned * dp_count * vocab_count
    col_new = DECAY_RATE * col_moment + (1.0 - DECAY_RATE) * (totals[0, :features] / vocab_rows)
    row_mean = totals[0, features] / vocab_rows
    row_new = row_new_all[:, 0]
    by_col = lax.rsqrt(col_new)[None, :]
    by_row = lax.rsqrt(row_new / row_mean)[:, None]
    direction = (grad[:owned] * by_row[:owned] * by_col).astype(BF16)
    wanted_step = grad[owned:] * by_row[owned:] * by_col
    fresh = (wanted_master - STEP_SCALE * wanted_step).astype(BF16)
    fresh = jnp.pad(fresh, ((0, 24 - used), (0, 0)))
    all_fresh = lax.all_gather(fresh, VOCAB, axis=0, tiled=True)
    spread = (
        (block_of * 24 + slot_of)[:, None]
        == jnp.arange(24 * vocab_count, dtype=jnp.int32)[None, :]
    ).astype(BF16)
    next_rows = jnp.dot(spread, all_fresh, preferred_element_type=F32).astype(BF16)
    return direction, row_new[:owned], col_new, next_rows


def solution(mesh):
    sizes = {"y": 4, "z": 8, "x": 4, "c": 2}
    fine = Mesh(mesh.devices.reshape(4, 8, 4, 2), ("y", "z", "x", "c"))
    rows = VOCAB + DP
    in_specs = (
        P(DP, VOCAB),
        P(DP, None),
        P(DP, None),
        P(DP),
        P(DP, None),
        P(DP, None),
        P(),
        P(rows, None),
        P(rows),
        P(),
    )
    out_specs = (P(rows, None), P(rows), P(), P(DP, None))
    return jax.shard_map(
        functools.partial(body, sizes),
        mesh=fine,
        in_specs=in_specs,
        out_specs=out_specs,
        check_vma=False,
    )
```
